32 devices in a mesh: seq: 8 (over z, x), head: 4 (over y, core).
Axes of the slice: x: 2, y: 2, z: 4, core: 2. Of those that a mesh axis runs over, the one named last changes fastest.
Arguments:
- queries: bfloat16 [1024, 1536], P('seq', 'head'), may hold values from -8 to 8
- cell_types: int32 [1024], P('seq'), may hold values from 0 to 127
- promoters: int32 [1024], P('seq'), may hold values from 0 to 16383, as said below
- offsets: int32 [1024], P('seq'), may hold values from -64 to 64, as said below
- cell_embed: bfloat16 [128, 1536], P(None, 'head'), may hold values from -3 to 3
- bin_keys: bfloat16 [16384, 1536], P('seq', 'head'), may hold values from -6 to 6
- bin_values: bfloat16 [16384, 1536], P('seq', 'head'), may hold values from -6 to 6
- slopes: float32 [16], P('head'), may hold values from 1.280082e-05 to 0.05
- w_out: bfloat16 [1536, 1536], P('head'), may hold values from -0.15625 to 0.15625
Outputs:
- pooled_features: bfloat16 [1024, 1536], P('seq', 'head')
The draws below stay inside these ranges and needn't reach their ends.
Inputs may be any that keep to these rules, and one draw needn't show every extreme that they name: `promoters`: the promoter of row r lies in bins (r // 128) * 2048 to (r // 128 + 1) * 2048 - 1; in each aligned block of 128 rows, the block's first row sits at the first of those bins and its second row at the last. `offsets`: in each aligned block of 128 rows the first row has offset -64 and the second row 64.
All inputs are finite; a program needn't handle non-finite values.
Results may differ from the reference program's by a relative error of at most 0.012.
Values may be sent and summed in bfloat16 or wider, within the bound.
A program may use at most 128 MiB of HBM per device.

```python
import math
import jax
import jax.numpy as jnp
from jax import lax

HEADS = 16
HEAD_DIM = 96
D = 1536
CT = 128
BIN_DEV = 2048
Q_DEV = 128
RADIUS = 7812
SHIFT = 64
HOPS = 4
BINS = 16384
Q_ALL = 1024
N_SEQ = 8


def positions(key):
    base = jax.random.fold_in(key, 7101)
    first, second, third = jax.random.split(base, 3)
    index = jnp.arange(Q_ALL, dtype=jnp.int32)
    block = index // Q_DEV
    within = index % Q_DEV
    inner = jnp.minimum(jax.random.randint(first, (Q_ALL,), 0, BIN_DEV), jax.random.randint(second, (Q_ALL,), 0, BIN_DEV))
    inner = jnp.where(within == 0, 0, jnp.where(within == 1, BIN_DEV - 1, inner))
    shifts = jax.random.randint(third, (Q_ALL,), -SHIFT, SHIFT + 1)
    shifts = jnp.where(within == 0, -SHIFT, jnp.where(within == 1, SHIFT, shifts))
    return ((block * BIN_DEV + inner).astype(jnp.int32), shifts.astype(jnp.int32))


def draw_promoters(key, part):
    return positions(key)[0]


def draw_offsets(key, part):
    return positions(key)[1]


def draw_bin_keys(key, part):
    inner_key = jax.random.fold_in(key, 7202)
    table = jnp.clip(jax.random.normal(inner_key, (BINS, D)), -6.0, 6.0)
    return table.astype(jnp.bfloat16)


def draw_queries(key, part):
    inner_key = jax.random.fold_in(key, 7303)
    table = jnp.clip(jax.random.normal(inner_key, (Q_ALL, D)), -6.0, 6.0)
    return table.astype(jnp.bfloat16)


def set_ends(entries, rng, least, largest):
    place = [jax.random.randint(jax.random.fold_in(rng, axis), (), 0, length) for axis, length in enumerate(entries.shape)]
    main_axis = entries.shape.index(max(entries.shape))
    neighbour = place[:main_axis] + [(place[main_axis] + 1) % entries.shape[main_axis]] + place[main_axis + 1:]
    return entries.at[tuple(place)].set(least).at[tuple(neighbour)].set(largest)


def block_scale(stream_key, dims, pieces, least, largest):
    level, own = 1.0, jax.random.fold_in(stream_key, 6)
    for dim, shards_of in pieces:
        steps = jnp.exp(jax.random.uniform(jax.random.fold_in(own, dim), (shards_of,), jnp.float32, least / len(pieces), largest / len(pieces)))
        level = level * jnp.repeat(steps, dims[dim] // shards_of).reshape([-1 if axis == dim else 1 for axis in range(len(dims))])
    return level


def noise(stream_key, extent, spread, reach, cuts=(), kind=jnp.bfloat16):
    loudness = block_scale(stream_key, extent, cuts, -0.22, 0.18) if cuts else 1.0
    entries = jax.random.normal(stream_key, extent, jnp.float32) * spread * loudness
    return jnp.minimum(jnp.maximum(entries, -reach), reach).astype(kind)


def setup_inputs(seed: int = 0) -> dict:
    seeds = jax.random.split(jax.random.key(seed), 10)
    queries = draw_queries(jax.random.fold_in(seeds[9], 71), 0)
    cell_types = set_ends(jax.random.randint(seeds[1], (Q_ALL,), 0, CT), jax.random.fold_in(seeds[1], 1), 0, CT - 1).astype(jnp.int32)
    promoters = draw_promoters(jax.random.fold_in(seeds[9], 71), 0)
    offsets = draw_offsets(jax.random.fold_in(seeds[9], 71), 0)
    cell_embed = noise(seeds[4], (CT, D), 0.5, 3.0, ((1, 4),))
    bin_keys = draw_bin_keys(jax.random.fold_in(seeds[9], 71), 0)
    bin_values = noise(seeds[6], (BINS, D), 1.0, 6.0, ((0, 8), (1, 4)))
    slopes = jnp.clip(jnp.exp(math.log(0.05) - 8.270269 * jax.random.uniform(seeds[7], (HEADS,), jnp.float32) ** block_scale(seeds[7], (HEADS,), ((0, 4),), -0.2, 0.2)), 1.2800819604308344e-05, 0.05)
    w_out = noise(seeds[8], (D, D), D ** -0.5, 0.15625, ((0, 4),))
    return dict(queries=queries, cell_types=cell_types, promoters=promoters, offsets=offsets, cell_embed=cell_embed, bin_keys=bin_keys, bin_values=bin_values, slopes=slopes, w_out=w_out)


def reference(queries, cell_types, promoters, offsets, cell_embed, bin_keys, bin_values, slopes, w_out):
    embedded = cell_embed.astype(jnp.float32)[cell_types]
    query_rows = (queries.astype(jnp.float32) + embedded).astype(jnp.bfloat16)
    centres = promoters + offsets
    padding = HOPS * BIN_DEV
    keys_padded = jnp.pad(bin_keys, ((padding, padding), (0, 0)))
    values_padded = jnp.pad(bin_values, ((padding, padding), (0, 0)))
    window_len = (2 * HOPS + 1) * BIN_DEV
    scale = HEAD_DIM ** -0.5

    def one_shard(shard):
        shard_rows = lax.dynamic_slice_in_dim(query_rows, shard * Q_DEV, Q_DEV, 0)
        shard_centres = lax.dynamic_slice_in_dim(centres, shard * Q_DEV, Q_DEV, 0)
        shard_keys = lax.dynamic_slice_in_dim(keys_padded, shard * BIN_DEV, window_len, 0)
        shard_values = lax.dynamic_slice_in_dim(values_padded, shard * BIN_DEV, window_len, 0)
        bin_index = (shard - HOPS) * BIN_DEV + jnp.arange(window_len, dtype=jnp.int32)
        distance = jnp.abs(bin_index[None, :] - shard_centres[:, None])
        usable = (distance <= RADIUS) & (bin_index[None, :] >= 0) & (bin_index[None, :] < BINS)
        distance_float = distance.astype(jnp.float32)
        head_queries = shard_rows.reshape(Q_DEV, HEADS, HEAD_DIM).transpose(1, 0, 2)
        head_keys = shard_keys.reshape(window_len, HEADS, HEAD_DIM).transpose(1, 0, 2)
        head_values = shard_values.reshape(window_len, HEADS, HEAD_DIM).transpose(1, 0, 2)

        def one_head(inputs):
            query_head, key_head, value_head, slope = inputs
            scores = jnp.dot(query_head, key_head.T, preferred_element_type=jnp.float32) * scale
            scores = scores - slope * distance_float
            scores = jnp.where(usable, scores, -1e30)
            row_max = jnp.max(scores, axis=1, keepdims=True)
            exps = jnp.where(usable, jnp.exp(scores - row_max), 0.0)
            totals = jnp.sum(exps, axis=1)
            weights = exps.astype(jnp.bfloat16)
            pooled_head = jnp.dot(weights, value_head, preferred_element_type=jnp.float32)
            return pooled_head / totals[:, None]

        pooled_heads = lax.map(one_head, (head_queries, head_keys, head_values, slopes))
        return pooled_heads.transpose(1, 0, 2).reshape(Q_DEV, D).astype(jnp.bfloat16)

    pooled = lax.map(one_shard, jnp.arange(N_SEQ, dtype=jnp.int32)).reshape(Q_ALL, D)
    return jnp.dot(pooled, w_out, preferred_element_type=jnp.float32).astype(jnp.bfloat16)
```

```python
import functools

import jax
import jax.numpy as jnp
from jax import lax
from jax.experimental import pallas as pl
from jax.experimental.pallas import tpu as pltpu
from jax.sharding import PartitionSpec as P

HEAD_DIM = 96
RADIUS = 7812
SHIFT = 64
HOPS = 4
LANES = 128
CHUNK = 256
EXTRA = 16
LOG2E = 1.4426950408889634
FAR = -1e30


def shift_by(value, by):
    peers = lax.axis_size("seq")
    pairs = [(i, i + by) for i in range(peers) if 0 <= i + by < peers]
    return lax.ppermute(value, "seq", pairs)


def identity_mask(size):
    return lax.broadcasted_iota(jnp.int32, (size, size), 0) == lax.broadcasted_iota(
        jnp.int32, (size, size), 1
    )


def as_column(row):
    size = row.shape[1]
    return jnp.sum(jnp.where(identity_mask(size), row, 0.0), axis=1, keepdims=True)


def as_row(column):
    size = column.shape[0]
    return jnp.sum(jnp.where(identity_mask(size), column, 0.0), axis=0, keepdims=True)


def tiles_of(head):
    first = head * HEAD_DIM
    start = first // LANES * LANES
    stop = -(-(first + HEAD_DIM) // LANES) * LANES
    return first, start, stop


def attend(hop, sign, pack, k_ref, v_ref, slope_ref, score_ref, out_ref, stat_ref):
    bins = k_ref.shape[0]
    rows = pack.shape[0] - EXTRA
    width = k_ref.shape[1]
    groups = width // HEAD_DIM
    corner = pack[rows:, :rows].astype(jnp.float32)
    within = as_column(corner[0:1] * 256.0 + corner[1:2])
    signf = sign.astype(jnp.float32)
    parts = {}
    for head in range(groups):
        first, start, stop = tiles_of(head)
        slope = slope_ref[head] * LOG2E
        lane = lax.broadcasted_iota(jnp.int32, (rows, stop - start), 1) + start
        query = pack[:rows, start:stop]
        query = jnp.where((lane >= first) & (lane < first + HEAD_DIM), query, jnp.zeros_like(query))
        slot = head % 2
        top = None
        if hop is None:
            ahead = signf * bins - within
        else:
            ahead = hop * bins - signf * within
        for begin in range(0, bins, CHUNK):
            raw = lax.dot_general(
                query,
                k_ref[begin : begin + CHUNK, start:stop],
                (((1,), (1,)), ((), ())),
                preferred_element_type=jnp.float32,
            )
            index = (lax.broadcasted_iota(jnp.int32, (1, CHUNK), 1) + begin).astype(jnp.float32)
            scaled = raw * (LOG2E * HEAD_DIM**-0.5)
            if hop is None:
                score = scaled - slope * jnp.abs(index + ahead)
                if 2 * bins - 1 + SHIFT > RADIUS:
                    score = jnp.where(jnp.abs(index + ahead) <= RADIUS, score, FAR)
            else:
                signed = index * signf
                score = scaled - slope * signed
                if (hop + 1) * bins - 1 + SHIFT > RADIUS:
                    score = jnp.where(signed <= RADIUS - ahead, score, FAR)
            score_ref[slot, :, begin : begin + CHUNK] = score
            for lanes in range(0, CHUNK, LANES):
                piece = score[:, lanes : lanes + LANES]
                top = piece if top is None else jnp.maximum(top, piece)
        peak = jnp.maximum(jnp.max(top, axis=1, keepdims=True), 0.1 * FAR)
        total = None
        gained = None
        for begin in range(0, bins, CHUNK):
            exps = jnp.exp2(score_ref[slot, :, begin : begin + CHUNK] - peak)
            for lanes in range(0, CHUNK, LANES):
                piece = exps[:, lanes : lanes + LANES]
                total = piece if total is None else total + piece
            term = jnp.dot(
                exps.astype(jnp.bfloat16),
                v_ref[begin : begin + CHUNK, start:stop],
                preferred_element_type=jnp.float32,
            )
            gained = term if gained is None else gained + term
        if hop is not None:
            peak = peak - slope * ahead
        stat_ref[head : head + 1, :] = as_row(peak)
        stat_ref[groups + head : groups + head + 1, :] = as_row(
            jnp.sum(total, axis=1, keepdims=True)
        )
        for tile in range(start, stop, LANES):
            parts.setdefault(tile, []).append((first, gained[:, tile - start : tile - start + LANES]))
    for tile, pieces in parts.items():
        lane = lax.broadcasted_iota(jnp.int32, (rows, LANES), 1) + tile
        value = pieces[0][1]
        for first, piece in pieces[1:]:
            value = jnp.where(lane >= first, piece, value)
        out_ref[:, tile : tile + LANES] = value.astype(jnp.bfloat16)


def attend_kernel(hops, seq_count, *refs):
    packs = refs[: 2 * hops + 1]
    k_ref, v_ref, slope_ref, out_ref, stat_ref, score_ref, pack_ref = refs[2 * hops + 1 :]
    position = lax.axis_index("seq")
    for slot in range(2 * hops + 1):
        pack_ref[slot] = packs[slot][...]

    def run(hop, shift):
        anchor = position - shift
        slot = shift + hops

        @pl.when((anchor >= 0) & (anchor < seq_count))
        def _():
            sign = shift if hop is None else jnp.where(shift > 0, 1, -1)
            attend(
                hop, sign, pack_ref.at[slot], k_ref, v_ref, slope_ref, score_ref,
                out_ref.at[slot], stat_ref.at[slot],
            )

    def near(i, _):
        run(None, i - 1)
        return 0

    lax.fori_loop(0, 3, near, 0)
    for hop in range(2, hops + 1):

        def far(i, _, hop=hop):
            run(hop, (2 * i - 1) * hop)
            return 0

        lax.fori_loop(0, 2, far, 0)


def local(queries, cell_types, promoters, offsets, cell_embed, bin_keys, bin_values, slopes, w_out):
    seq_count = lax.axis_size("seq")
    position = lax.axis_index("seq")
    bins = bin_keys.shape[0]
    rows, width = queries.shape
    groups = slopes.shape[0]
    hops = min(HOPS, seq_count - 1)
    one_hot = (
        cell_types[:, None] == jnp.arange(cell_embed.shape[0], dtype=jnp.int32)[None, :]
    ).astype(jnp.bfloat16)
    embedded = jnp.dot(one_hot, cell_embed, preferred_element_type=jnp.float32)
    query_rows = (queries.astype(jnp.float32) + embedded).astype(jnp.bfloat16)
    within = promoters + offsets - position * bins
    high = jnp.floor_divide(within, 256)
    corner = jnp.stack([high, within - 256 * high]).astype(jnp.bfloat16)
    pack = jnp.concatenate(
        [query_rows, jnp.pad(corner, ((0, EXTRA - 2), (0, width - rows)))], axis=0
    )
    packs = [pack if d == 0 else shift_by(pack, d) for d in range(-hops, hops + 1)]
    slots = 2 * hops + 1
    vmem = pl.BlockSpec(memory_space=pltpu.VMEM)
    outs, stats = pl.pallas_call(
        functools.partial(attend_kernel, hops, seq_count),
        out_shape=(
            jax.ShapeDtypeStruct((slots, rows, width), jnp.bfloat16),
            jax.ShapeDtypeStruct((slots, 2 * groups, rows), jnp.float32),
        ),
        in_specs=[vmem] * (slots + 2) + [pl.BlockSpec(memory_space=pltpu.SMEM)],
        out_specs=(vmem, vmem),
        scratch_shapes=[
            pltpu.VMEM((2, rows, bins), jnp.float32),
            pltpu.VMEM((slots, rows + EXTRA, width), jnp.bfloat16),
        ],
    )(*packs, bin_keys, bin_values, slopes)
    peaks, totals, sums = [], [], []
    for d in range(-hops, hops + 1):
        back_out = outs[d + hops] if d == 0 else shift_by(outs[d + hops], -d)
        back_stat = stats[d + hops] if d == 0 else shift_by(stats[d + hops], -d)
        there = (position + d >= 0) & (position + d < seq_count)
        peaks.append(jnp.where(there, back_stat[:groups], FAR))
        totals.append(jnp.where(there, back_stat[groups:], 0.0))
        sums.append(jnp.where(there, back_out, 0))
    peak = functools.reduce(jnp.maximum, peaks)
    total, pooled = 0.0, 0.0
    for p, t, s in zip(peaks, totals, sums):
        factor = jnp.exp2(p - peak)
        total = total + factor * t
        pooled = pooled + s.astype(jnp.float32).reshape(rows, groups, HEAD_DIM) * factor.T[:, :, None]
    pooled = (pooled / total.T[:, :, None]).reshape(rows, width).astype(jnp.bfloat16)
    partial_sums = jnp.dot(pooled, w_out, preferred_element_type=jnp.float32)
    return lax.psum_scatter(
        partial_sums.astype(jnp.bfloat16), "head", scatter_dimension=1, tiled=True
    )


def solution(mesh):
    return jax.shard_map(
        local,
        mesh=mesh,
        in_specs=(
            P("seq", "head"),
            P("seq"),
            P("seq"),
            P("seq"),
            P(None, "head"),
            P("seq", "head"),
            P("seq", "head"),
            P("head"),
            P("head", None),
        ),
        out_specs=P("seq", "head"),
        check_vma=False,
    )
```

```python
import functools

import jax
import jax.numpy as jnp
from jax import lax
from jax.experimental import pallas as pl
from jax.experimental.pallas import tpu as pltpu
from jax.sharding import PartitionSpec as P

HEAD_DIM = 96
RADIUS = 7812
SHIFT = 64
HOPS = 4
LANES = 128
CHUNK = 256
EXTRA = 16
LOG2E = 1.4426950408889634
FAR = -1e30


MESH = pl.DeviceIdType.MESH


def identity_mask(size):
    return lax.broadcasted_iota(jnp.int32, (size, size), 0) == lax.broadcasted_iota(
        jnp.int32, (size, size), 1
    )


def as_column(row):
    size = row.shape[1]
    return jnp.sum(jnp.where(identity_mask(size), row, 0.0), axis=1, keepdims=True)


def as_row(column):
    size = column.shape[0]
    return jnp.sum(jnp.where(identity_mask(size), column, 0.0), axis=0, keepdims=True)


def tiles_of(head):
    first = head * HEAD_DIM
    start = first // LANES * LANES
    stop = -(-(first + HEAD_DIM) // LANES) * LANES
    return first, start, stop


def attend(hop, sign, pack, k_ref, v_ref, slope_ref, score_ref, out_ref, stat_ref):
    bins = k_ref.shape[0]
    rows = pack.shape[0] - EXTRA
    width = k_ref.shape[1]
    groups = width // HEAD_DIM
    corner = pack[rows:, :rows].astype(jnp.float32)
    within = as_column(corner[0:1] * 256.0 + corner[1:2])
    signf = sign.astype(jnp.float32)
    parts = {}
    for head in range(groups):
        first, start, stop = tiles_of(head)
        slope = slope_ref[head] * LOG2E
        lane = lax.broadcasted_iota(jnp.int32, (rows, stop - start), 1) + start
        query = pack[:rows, start:stop]
        query = jnp.where((lane >= first) & (lane < first + HEAD_DIM), query, jnp.zeros_like(query))
        slot = head % 2
        top = None
        if hop is None:
            ahead = signf * bins - within
        else:
            ahead = hop * bins - signf * within
        for begin in range(0, bins, CHUNK):
            raw = lax.dot_general(
                query,
                k_ref[begin : begin + CHUNK, start:stop],
                (((1,), (1,)), ((), ())),
                preferred_element_type=jnp.float32,
            )
            index = (lax.broadcasted_iota(jnp.int32, (1, CHUNK), 1) + begin).astype(jnp.float32)
            scaled = raw * (LOG2E * HEAD_DIM**-0.5)
            if hop is None:
                score = scaled - slope * jnp.abs(index + ahead)
                if 2 * bins - 1 + SHIFT > RADIUS:
                    score = jnp.where(jnp.abs(index + ahead) <= RADIUS, score, FAR)
            else:
                signed = index * signf
                score = scaled - slope * signed
                if (hop + 1) * bins - 1 + SHIFT > RADIUS:
                    score = jnp.where(signed <= RADIUS - ahead, score, FAR)
            score_ref[slot, :, begin : begin + CHUNK] = score
            for lanes in range(0, CHUNK, LANES):
                piece = score[:, lanes : lanes + LANES]
                top = piece if top is None else jnp.maximum(top, piece)
        peak = jnp.maximum(jnp.max(top, axis=1, keepdims=True), 0.1 * FAR)
        total = None
        gained = None
        for begin in range(0, bins, CHUNK):
            exps = jnp.exp2(score_ref[slot, :, begin : begin + CHUNK] - peak)
            for lanes in range(0, CHUNK, LANES):
                piece = exps[:, lanes : lanes + LANES]
                total = piece if total is None else total + piece
            term = jnp.dot(
                exps.astype(jnp.bfloat16),
                v_ref[begin : begin + CHUNK, start:stop],
                preferred_element_type=jnp.float32,
            )
            gained = term if gained is None else gained + term
        if hop is not None:
            peak = peak - slope * ahead
        stat_ref[head : head + 1, :] = as_row(peak)
        stat_ref[groups + head : groups + head + 1, :] = as_row(
            jnp.sum(total, axis=1, keepdims=True)
        )
        for tile in range(start, stop, LANES):
            parts.setdefault(tile, []).append((first, gained[:, tile - start : tile - start + LANES]))
    for tile, pieces in parts.items():
        lane = lax.broadcasted_iota(jnp.int32, (rows, LANES), 1) + tile
        value = pieces[0][1]
        for first, piece in pieces[1:]:
            value = jnp.where(lane >= first, piece, value)
        out_ref[:, tile : tile + LANES] = value.astype(jnp.bfloat16)


def attend_kernel(
    hops, seq_count, head_count,
    pack_in, k_hbm, v_hbm, w_hbm, slope_ref, result_ref,
    k_ref, v_ref, w_ref, pack_ref, out_ref, stat_ref, back_ref, back_stat_ref,
    score_ref, sum_ref, part_ref, head_ref,
    load_sem, q_send, q_recv, o_send, o_recv, s_send, s_recv, h_send, h_recv,
):
    position = lax.axis_index("seq")
    mine = lax.axis_index("head")
    rows, width = out_ref.shape[1:]
    groups = width // HEAD_DIM
    piece = result_ref.shape[1]
    loads = [
        pltpu.make_async_copy(src, dst, load_sem.at[i])
        for i, (src, dst) in enumerate(((k_hbm, k_ref), (v_hbm, v_ref), (w_hbm, w_ref)))
    ]
    for load in loads:
        load.start()

    def inside(index):
        return (index >= 0) & (index < seq_count)

    barrier = pltpu.get_barrier_semaphore()
    offsets = [sign * hop for hop in range(1, hops + 1) for sign in (1, -1)]
    for d in offsets:

        @pl.when(inside(position + d))
        def _(d=d):
            pl.semaphore_signal(
                barrier, inc=1, device_id=(position + d, mine), device_id_type=MESH
            )

    for r in range(1, head_count):
        pl.semaphore_signal(
            barrier, inc=1, device_id=(position, lax.rem(mine + r, head_count)), device_id_type=MESH
        )
    around = jnp.minimum(position, hops) + jnp.minimum(seq_count - 1 - position, hops)
    pl.semaphore_wait(barrier, around + head_count - 1)

    def query_copy(slot, target):
        return pltpu.make_async_remote_copy(
            src_ref=pack_in, dst_ref=pack_ref.at[slot], send_sem=q_send.at[slot],
            recv_sem=q_recv.at[slot], device_id=(target, mine), device_id_type=MESH,
        )

    def out_copy(slot, target):
        return pltpu.make_async_remote_copy(
            src_ref=out_ref.at[slot], dst_ref=back_ref.at[slot], send_sem=o_send.at[slot],
            recv_sem=o_recv.at[slot], device_id=(target, mine), device_id_type=MESH,
        )

    def stat_copy(slot, target):
        return pltpu.make_async_remote_copy(
            src_ref=stat_ref.at[slot], dst_ref=back_stat_ref.at[slot], send_sem=s_send.at[slot],
            recv_sem=s_recv.at[slot], device_id=(target, mine), device_id_type=MESH,
        )

    order = [1] + list(range(hops, 1, -1))
    for hop in order:
        for d in (hop, -hop):

            @pl.when(inside(position + d))
            def _(d=d):
                query_copy(d + hops, position + d).start()

    pack_ref[hops] = pack_in[...]
    loads[0].wait()
    loads[1].wait()

    def run(hop, shift):
        anchor = position - shift
        slot = shift + hops

        @pl.when(inside(anchor))
        def _():
            sign = shift if hop is None else jnp.where(shift > 0, 1, -1)

            @pl.when(shift != 0)
            def _():
                query_copy(slot, anchor).wait_recv()

            attend(
                hop, sign, pack_ref.at[slot], k_ref, v_ref, slope_ref, score_ref,
                out_ref.at[slot], stat_ref.at[slot],
            )

            @pl.when(shift != 0)
            def _():
                stat_copy(slot, anchor).start()
                out_copy(slot, anchor).start()

    def near(i, _):
        run(None, i - 3 * (i // 2))
        return 0

    lax.fori_loop(0, 3, near, 0)
    for hop in order[1:]:

        def far(i, _, hop=hop):
            run(hop, (2 * i - 1) * hop)
            return 0

        lax.fori_loop(0, 2, far, 0)

    back_stat_ref[hops] = stat_ref[hops]
    for d in offsets:
        slot = d + hops

        @pl.when(inside(position + d))
        def _(d=d, slot=slot):
            stat_copy(slot, position + d).wait_recv()

        @pl.when(jnp.logical_not(inside(position + d)))
        def _(slot=slot):
            back_stat_ref[slot, :groups, :] = jnp.full((groups, rows), FAR, jnp.float32)
            back_stat_ref[slot, groups:, :] = jnp.zeros((groups, rows), jnp.float32)

    slots = 2 * hops + 1
    peak = back_stat_ref[0, :groups, :]
    for slot in range(1, slots):
        peak = jnp.maximum(peak, back_stat_ref[slot, :groups, :])
    factors = [jnp.exp2(back_stat_ref[slot, :groups, :] - peak) for slot in range(slots)]
    total = factors[0] * back_stat_ref[0, groups:, :]
    for slot in range(1, slots):
        total = total + factors[slot] * back_stat_ref[slot, groups:, :]
    lane = lax.broadcasted_iota(jnp.int32, (rows, width), 1)

    def spread(factor):
        columns = factor.T
        wide = columns[:, 0:1]
        for head in range(1, groups):
            wide = jnp.where(lane >= head * HEAD_DIM, columns[:, head : head + 1], wide)
        return wide

    sum_ref[...] = out_ref[hops].astype(jnp.float32) * spread(factors[hops] / total)
    for d in offsets:
        slot = d + hops

        @pl.when(inside(position + d))
        def _(d=d, slot=slot):
            out_copy(slot, position + d).wait_recv()
            sum_ref[...] += back_ref[slot].astype(jnp.float32) * spread(factors[slot] / total)

    pooled = sum_ref[...].astype(jnp.bfloat16)
    loads[2].wait()

    def head_copy(r, target):
        return pltpu.make_async_remote_copy(
            src_ref=part_ref.at[r - 1], dst_ref=head_ref.at[r - 1], send_sem=h_send.at[r - 1],
            recv_sem=h_recv.at[r - 1], device_id=(position, target), device_id_type=MESH,
        )

    def share(target):
        columns = pl.ds(pl.multiple_of(target * piece, piece), piece)
        return jnp.dot(pooled, w_ref[:, columns], preferred_element_type=jnp.float32)

    for r in range(1, head_count):
        target = lax.rem(mine + r, head_count)
        part_ref[r - 1] = share(target).astype(jnp.bfloat16)
        head_copy(r, target).start()
    result = share(mine)
    for r in range(1, head_count):
        head_copy(r, lax.rem(mine + r, head_count)).wait_recv()
        result = result + head_ref[r - 1].astype(jnp.float32)
    result_ref[...] = result.astype(jnp.bfloat16)

    for r in range(1, head_count):
        head_copy(r, lax.rem(mine + r, head_count)).wait_send()
    for d in offsets:

        @pl.when(inside(position + d))
        def _(d=d):
            query_copy(d + hops, position + d).wait_send()

        @pl.when(inside(position - d))
        def _(d=d):
            stat_copy(d + hops, position - d).wait_send()
            out_copy(d + hops, position - d).wait_send()


def local(queries, cell_types, promoters, offsets, cell_embed, bin_keys, bin_values, slopes, w_out):
    seq_count = lax.axis_size("seq")
    position = lax.axis_index("seq")
    bins = bin_keys.shape[0]
    rows, width = queries.shape
    groups = slopes.shape[0]
    hops = min(HOPS, seq_count - 1)
    one_hot = (
        cell_types[:, None] == jnp.arange(cell_embed.shape[0], dtype=jnp.int32)[None, :]
    ).astype(jnp.bfloat16)
    embedded = jnp.dot(one_hot, cell_embed, preferred_element_type=jnp.float32)
    query_rows = (queries.astype(jnp.float32) + embedded).astype(jnp.bfloat16)
    within = promoters + offsets - position * bins
    high = jnp.floor_divide(within, 256)
    corner = jnp.stack([high, within - 256 * high]).astype(jnp.bfloat16)
    pack = jnp.concatenate(
        [query_rows, jnp.pad(corner, ((0, EXTRA - 2), (0, width - rows)))], axis=0
    )
    head_count = lax.axis_size("head")
    slots = 2 * hops + 1
    piece = w_out.shape[1] // head_count
    vmem = pl.BlockSpec(memory_space=pltpu.VMEM)
    anywhere = pl.BlockSpec(memory_space=pl.ANY)
    return pl.pallas_call(
        functools.partial(attend_kernel, hops, seq_count, head_count),
        out_shape=jax.ShapeDtypeStruct((rows, piece), jnp.bfloat16),
        in_specs=[vmem] + [anywhere] * 3 + [pl.BlockSpec(memory_space=pltpu.SMEM)],
        out_specs=vmem,
        scratch_shapes=[
            pltpu.VMEM((bins, width), jnp.bfloat16),
            pltpu.VMEM((bins, width), jnp.bfloat16),
            pltpu.VMEM(w_out.shape, jnp.bfloat16),
            pltpu.VMEM((slots, rows + EXTRA, width), jnp.bfloat16),
            pltpu.VMEM((slots, rows, width), jnp.bfloat16),
            pltpu.VMEM((slots, 2 * groups, rows), jnp.float32),
            pltpu.VMEM((slots, rows, width), jnp.bfloat16),
            pltpu.VMEM((slots, 2 * groups, rows), jnp.float32),
            pltpu.VMEM((2, rows, bins), jnp.float32),
            pltpu.VMEM((rows, width), jnp.float32),
            pltpu.VMEM((head_count - 1, rows, piece), jnp.bfloat16),
            pltpu.VMEM((head_count - 1, rows, piece), jnp.bfloat16),
            pltpu.SemaphoreType.DMA((3,)),
        ]
        + [pltpu.SemaphoreType.DMA((slots,))] * 6
        + [pltpu.SemaphoreType.DMA((head_count - 1,))] * 2,
        compiler_params=pltpu.CompilerParams(collective_id=0, has_side_effects=True),
    )(pack, bin_keys, bin_values, w_out, slopes)


def solution(mesh):
    return jax.shard_map(
        local,
        mesh=mesh,
        in_specs=(
            P("seq", "head"),
            P("seq"),
            P("seq"),
            P("seq"),
            P(None, "head"),
            P("seq", "head"),
            P("seq", "head"),
            P("head"),
            P("head", None),
        ),
        out_specs=P("seq", "head"),
        check_vma=False,
    )
```

```python
import functools

import jax
import jax.numpy as jnp
from jax import lax
from jax.experimental import pallas as pl
from jax.experimental.pallas import tpu as pltpu
from jax.sharding import PartitionSpec as P

HEAD_DIM = 96
RADIUS = 7812
SHIFT = 64
HOPS = 4
LANES = 128
CHUNK = 256
EXTRA = 16
LOG2E = 1.4426950408889634
FAR = -1e30


MESH = pl.DeviceIdType.MESH


def identity_mask(size):
    return lax.broadcasted_iota(jnp.int32, (size, size), 0) == lax.broadcasted_iota(
        jnp.int32, (size, size), 1
    )


def as_column(row):
    size = row.shape[1]
    return jnp.sum(jnp.where(identity_mask(size), row, 0.0), axis=1, keepdims=True)


def as_row(column):
    size = column.shape[0]
    return jnp.sum(jnp.where(identity_mask(size), column, 0.0), axis=0, keepdims=True)


def tiles_of(head):
    first = head * HEAD_DIM
    start = first // LANES * LANES
    stop = -(-(first + HEAD_DIM) // LANES) * LANES
    return first, start, stop


def attend(hop, sign, pack, k_ref, v_ref, slope_ref, score_ref, out_ref, stat_ref):
    bins = k_ref.shape[0]
    rows = pack.shape[0] - EXTRA
    width = k_ref.shape[1]
    groups = width // HEAD_DIM
    corner = pack[rows:, :rows].astype(jnp.float32)
    within = as_column(corner[0:1] * 256.0 + corner[1:2])
    signf = sign.astype(jnp.float32)
    parts = {}
    for head in range(groups):
        first, start, stop = tiles_of(head)
        slope = slope_ref[head] * LOG2E
        lane = lax.broadcasted_iota(jnp.int32, (rows, stop - start), 1) + start
        query = pack[:rows, start:stop]
        query = jnp.where((lane >= first) & (lane < first + HEAD_DIM), query, jnp.zeros_like(query))
        slot = head % 2
        top = None
        if hop is None:
            ahead = signf * bins - within
        else:
            ahead = hop * bins - signf * within
        for begin in range(0, bins, CHUNK):
            raw = lax.dot_general(
                query,
                k_ref[begin : begin + CHUNK, start:stop],
                (((1,), (1,)), ((), ())),
                preferred_element_type=jnp.float32,
            )
            index = (lax.broadcasted_iota(jnp.int32, (1, CHUNK), 1) + begin).astype(jnp.float32)
            scaled = raw * (LOG2E * HEAD_DIM**-0.5)
            if hop is None:
                score = scaled - slope * jnp.abs(index + ahead)
                if 2 * bins - 1 + SHIFT > RADIUS:
                    score = jnp.where(jnp.abs(index + ahead) <= RADIUS, score, FAR)
            else:
                signed = index * signf
                score = scaled - slope * signed
                if (hop + 1) * bins - 1 + SHIFT > RADIUS:
                    score = jnp.where(signed <= RADIUS - ahead, score, FAR)
            score_ref[slot, :, begin : begin + CHUNK] = score
            for lanes in range(0, CHUNK, LANES):
                piece = score[:, lanes : lanes + LANES]
                top = piece if top is None else jnp.maximum(top, piece)
        peak = jnp.maximum(jnp.max(top, axis=1, keepdims=True), 0.1 * FAR)
        total = None
        gained = None
        for begin in range(0, bins, CHUNK):
            exps = jnp.exp2(score_ref[slot, :, begin : begin + CHUNK] - peak)
            for lanes in range(0, CHUNK, LANES):
                piece = exps[:, lanes : lanes + LANES]
                total = piece if total is None else total + piece
            term = jnp.dot(
                exps.astype(jnp.bfloat16),
                v_ref[begin : begin + CHUNK, start:stop],
                preferred_element_type=jnp.float32,
            )
            gained = term if gained is None else gained + term
        if hop is not None:
            peak = peak - slope * ahead
        stat_ref[head : head + 1, :] = as_row(peak)
        stat_ref[groups + head : groups + head + 1, :] = as_row(
            jnp.sum(total, axis=1, keepdims=True)
        )
        for tile in range(start, stop, LANES):
            parts.setdefault(tile, []).append((first, gained[:, tile - start : tile - start + LANES]))
    for tile, pieces in parts.items():
        lane = lax.broadcasted_iota(jnp.int32, (rows, LANES), 1) + tile
        value = pieces[0][1]
        for first, piece in pieces[1:]:
            value = jnp.where(lane >= first, piece, value)
        out_ref[:, tile : tile + LANES] = value.astype(jnp.bfloat16)


def attend_kernel(
    hops, seq_count, head_count,
    query_ref, type_ref, promoter_ref, offset_ref, embed_ref, k_hbm, v_hbm, w_hbm, slope_ref,
    result_ref,
    k_ref, v_ref, w_ref, pack_ref, out_ref, stat_ref, back_ref, back_stat_ref,
    score_ref, sum_ref, part_ref, head_ref,
    load_sem, q_send, q_recv, o_send, o_recv, s_send, s_recv, h_send, h_recv,
):
    position = lax.axis_index("seq")
    mine = lax.axis_index("head")
    rows, width = out_ref.shape[1:]
    groups = width // HEAD_DIM
    piece = result_ref.shape[1]
    loads = [
        pltpu.make_async_copy(src, dst, load_sem.at[i])
        for i, (src, dst) in enumerate(((k_hbm, k_ref), (v_hbm, v_ref), (w_hbm, w_ref)))
    ]
    for load in loads:
        load.start()

    def inside(index):
        return (index >= 0) & (index < seq_count)

    barrier = pltpu.get_barrier_semaphore()
    offsets = [sign * hop for hop in range(1, hops + 1) for sign in (1, -1)]
    for d in offsets:

        @pl.when(inside(position + d))
        def _(d=d):
            pl.semaphore_signal(
                barrier, inc=1, device_id=(position + d, mine), device_id_type=MESH
            )

    for r in range(1, head_count):
        pl.semaphore_signal(
            barrier, inc=1, device_id=(position, lax.rem(mine + r, head_count)), device_id_type=MESH
        )

    bins = k_ref.shape[0]
    chosen = (
        lax.broadcasted_iota(jnp.int32, (embed_ref.shape[0], rows), 0) == type_ref[...]
    ).astype(jnp.float32)
    embedded = jnp.dot(
        chosen.T.astype(jnp.bfloat16), embed_ref[...], preferred_element_type=jnp.float32
    )
    home = pack_ref.at[hops]
    home[:rows, :] = (query_ref[...].astype(jnp.float32) + embedded).astype(jnp.bfloat16)
    within = promoter_ref[...] + offset_ref[...] - position * bins
    high = lax.shift_right_arithmetic(within, 8)
    digit = lax.broadcasted_iota(jnp.int32, (EXTRA, rows), 0)
    corner = jnp.where(digit == 0, high, within - 256 * high).astype(jnp.float32)
    home[rows:, :] = jnp.zeros((EXTRA, width), jnp.bfloat16)
    home[rows:, :rows] = corner.astype(jnp.bfloat16)

    around = jnp.minimum(position, hops) + jnp.minimum(seq_count - 1 - position, hops)
    pl.semaphore_wait(barrier, around + head_count - 1)

    def query_copy(slot, target):
        return pltpu.make_async_remote_copy(
            src_ref=pack_ref.at[hops], dst_ref=pack_ref.at[slot], send_sem=q_send.at[slot],
            recv_sem=q_recv.at[slot], device_id=(target, mine), device_id_type=MESH,
        )

    def out_copy(slot, target):
        return pltpu.make_async_remote_copy(
            src_ref=out_ref.at[slot], dst_ref=back_ref.at[slot], send_sem=o_send.at[slot],
            recv_sem=o_recv.at[slot], device_id=(target, mine), device_id_type=MESH,
        )

    def stat_copy(slot, target):
        return pltpu.make_async_remote_copy(
            src_ref=stat_ref.at[slot], dst_ref=back_stat_ref.at[slot], send_sem=s_send.at[slot],
            recv_sem=s_recv.at[slot], device_id=(target, mine), device_id_type=MESH,
        )

    order = [1] + list(range(hops, 1, -1))
    for hop in order:
        for d in (hop, -hop):

            @pl.when(inside(position + d))
            def _(d=d):
                query_copy(d + hops, position + d).start()

    loads[0].wait()
    loads[1].wait()

    def run(hop, shift):
        anchor = position - shift
        slot = shift + hops

        @pl.when(inside(anchor))
        def _():
            sign = shift if hop is None else jnp.where(shift > 0, 1, -1)

            @pl.when(shift != 0)
            def _():
                query_copy(slot, anchor).wait_recv()

            attend(
                hop, sign, pack_ref.at[slot], k_ref, v_ref, slope_ref, score_ref,
                out_ref.at[slot], stat_ref.at[slot],
            )

            @pl.when(shift != 0)
            def _():
                stat_copy(slot, anchor).start()
                out_copy(slot, anchor).start()

    def near(i, _):
        run(None, i - 3 * (i // 2))
        return 0

    lax.fori_loop(0, 3, near, 0)
    for hop in order[1:]:

        def far(i, _, hop=hop):
            run(hop, (2 * i - 1) * hop)
            return 0

        lax.fori_loop(0, 2, far, 0)

    back_stat_ref[hops] = stat_ref[hops]
    for d in offsets:
        slot = d + hops

        @pl.when(inside(position + d))
        def _(d=d, slot=slot):
            stat_copy(slot, position + d).wait_recv()

        @pl.when(jnp.logical_not(inside(position + d)))
        def _(slot=slot):
            back_stat_ref[slot, :groups, :] = jnp.full((groups, rows), FAR, jnp.float32)
            back_stat_ref[slot, groups:, :] = jnp.zeros((groups, rows), jnp.float32)

    slots = 2 * hops + 1
    peak = back_stat_ref[0, :groups, :]
    for slot in range(1, slots):
        peak = jnp.maximum(peak, back_stat_ref[slot, :groups, :])
    factors = [jnp.exp2(back_stat_ref[slot, :groups, :] - peak) for slot in range(slots)]
    total = factors[0] * back_stat_ref[0, groups:, :]
    for slot in range(1, slots):
        total = total + factors[slot] * back_stat_ref[slot, groups:, :]
    lane = lax.broadcasted_iota(jnp.int32, (rows, width), 1)

    def spread(factor):
        columns = factor.T
        wide = columns[:, 0:1]
        for head in range(1, groups):
            wide = jnp.where(lane >= head * HEAD_DIM, columns[:, head : head + 1], wide)
        return wide

    sum_ref[...] = out_ref[hops].astype(jnp.float32) * spread(factors[hops] / total)
    for d in offsets:
        slot = d + hops

        @pl.when(inside(position + d))
        def _(d=d, slot=slot):
            out_copy(slot, position + d).wait_recv()
            sum_ref[...] += back_ref[slot].astype(jnp.float32) * spread(factors[slot] / total)

    pooled = sum_ref[...].astype(jnp.bfloat16)
    loads[2].wait()

    def head_copy(r, target):
        return pltpu.make_async_remote_copy(
            src_ref=part_ref.at[r - 1], dst_ref=head_ref.at[r - 1], send_sem=h_send.at[r - 1],
            recv_sem=h_recv.at[r - 1], device_id=(position, target), device_id_type=MESH,
        )

    def share(target):
        columns = pl.ds(pl.multiple_of(target * piece, piece), piece)
        return jnp.dot(pooled, w_ref[:, columns], preferred_element_type=jnp.float32)

    for r in range(1, head_count):
        target = lax.rem(mine + r, head_count)
        part_ref[r - 1] = share(target).astype(jnp.bfloat16)
        head_copy(r, target).start()
    result = share(mine)
    for r in range(1, head_count):
        head_copy(r, lax.rem(mine + r, head_count)).wait_recv()
        result = result + head_ref[r - 1].astype(jnp.float32)
    result_ref[...] = result

    for r in range(1, head_count):
        head_copy(r, lax.rem(mine + r, head_count)).wait_send()
    for d in offsets:

        @pl.when(inside(position + d))
        def _(d=d):
            query_copy(d + hops, position + d).wait_send()

        @pl.when(inside(position - d))
        def _(d=d):
            stat_copy(d + hops, position - d).wait_send()
            out_copy(d + hops, position - d).wait_send()


def local(queries, cell_types, promoters, offsets, cell_embed, bin_keys, bin_values, slopes, w_out):
    seq_count = lax.axis_size("seq")
    bins = bin_keys.shape[0]
    rows, width = queries.shape
    groups = slopes.shape[0]
    hops = min(HOPS, seq_count - 1)
    head_count = lax.axis_size("head")
    slots = 2 * hops + 1
    piece = w_out.shape[1] // head_count
    vmem = pl.BlockSpec(memory_space=pltpu.VMEM)
    anywhere = pl.BlockSpec(memory_space=pl.ANY)
    result = pl.pallas_call(
        functools.partial(attend_kernel, hops, seq_count, head_count),
        out_shape=jax.ShapeDtypeStruct((rows, piece), jnp.float32),
        in_specs=[vmem] * 5 + [anywhere] * 3 + [pl.BlockSpec(memory_space=pltpu.SMEM)],
        out_specs=vmem,
        scratch_shapes=[
            pltpu.VMEM((bins, width), jnp.bfloat16),
            pltpu.VMEM((bins, width), jnp.bfloat16),
            pltpu.VMEM(w_out.shape, jnp.bfloat16),
            pltpu.VMEM((slots, rows + EXTRA, width), jnp.bfloat16),
            pltpu.VMEM((slots, rows, width), jnp.bfloat16),
            pltpu.VMEM((slots, 2 * groups, rows), jnp.float32),
            pltpu.VMEM((slots, rows, width), jnp.bfloat16),
            pltpu.VMEM((slots, 2 * groups, rows), jnp.float32),
            pltpu.VMEM((2, rows, bins), jnp.float32),
            pltpu.VMEM((rows, width), jnp.float32),
            pltpu.VMEM((head_count - 1, rows, piece), jnp.bfloat16),
            pltpu.VMEM((head_count - 1, rows, piece), jnp.bfloat16),
            pltpu.SemaphoreType.DMA((3,)),
        ]
        + [pltpu.SemaphoreType.DMA((slots,))] * 6
        + [pltpu.SemaphoreType.DMA((head_count - 1,))] * 2,
        compiler_params=pltpu.CompilerParams(collective_id=0, has_side_effects=True),
    )(
        queries,
        cell_types[None],
        promoters[None],
        offsets[None],
        cell_embed,
        bin_keys,
        bin_values,
        w_out,
        slopes,
    )
    return result.astype(jnp.bfloat16)


def solution(mesh):
    return jax.shard_map(
        local,
        mesh=mesh,
        in_specs=(
            P("seq", "head"),
            P("seq"),
            P("seq"),
            P("seq"),
            P(None, "head"),
            P("seq", "head"),
            P("seq", "head"),
            P("head"),
            P("head", None),
        ),
        out_specs=P("seq", "head"),
        check_vma=False,
    )
```

```python
import functools

import jax
import jax.numpy as jnp
from jax import lax
from jax.experimental import pallas as pl
from jax.experimental.pallas import tpu as pltpu
from jax.sharding import PartitionSpec as P

HEAD_DIM = 96
RADIUS = 7812
SHIFT = 64
HOPS = 4
LANES = 128
CHUNK = 256
EXTRA = 16
LOG2E = 1.4426950408889634
FAR = -1e30


MESH = pl.DeviceIdType.MESH


def identity_mask(size):
    return lax.broadcasted_iota(jnp.int32, (size, size), 0) == lax.broadcasted_iota(
        jnp.int32, (size, size), 1
    )


def as_column(row):
    size = row.shape[1]
    return jnp.sum(jnp.where(identity_mask(size), row, 0.0), axis=1, keepdims=True)


def as_row(column):
    size = column.shape[0]
    return jnp.sum(jnp.where(identity_mask(size), column, 0.0), axis=0, keepdims=True)


def tiles_of(head):
    first = head * HEAD_DIM
    start = first // LANES * LANES
    stop = -(-(first + HEAD_DIM) // LANES) * LANES
    return first, start, stop


def attend(hop, signs, slots, pack_ref, k_ref, v_ref, slope_ref, score_ref, out_ref, stat_ref):
    bins = k_ref.shape[0]
    rows = pack_ref.shape[1] - EXTRA
    width = k_ref.shape[1]
    groups = width // HEAD_DIM
    count = len(signs)
    aheads = []
    for sign, slot in zip(signs, slots):
        corner = pack_ref[slot, rows:, :rows].astype(jnp.float32)
        within = as_column(corner[0:1] * 256.0 + corner[1:2])
        aheads.append(hop * bins - sign * within if hop >= 2 else sign * hop * bins - within)
    parts = [{} for _ in signs]
    for head in range(groups):
        first, start, stop = tiles_of(head)
        slope = slope_ref[head] * LOG2E
        lane = lax.broadcasted_iota(jnp.int32, (count * rows, stop - start), 1) + start
        query = [pack_ref[slot, :rows, start:stop] for slot in slots]
        query = jnp.concatenate(query, axis=0) if count > 1 else query[0]
        query = jnp.where((lane >= first) & (lane < first + HEAD_DIM), query, jnp.zeros_like(query))
        buffer = head % 2
        tops = [None] * count
        for begin in range(0, bins, CHUNK):
            raw = lax.dot_general(
                query,
                k_ref[begin : begin + CHUNK, start:stop],
                (((1,), (1,)), ((), ())),
                preferred_element_type=jnp.float32,
            )
            index = (lax.broadcasted_iota(jnp.int32, (1, CHUNK), 1) + begin).astype(jnp.float32)
            for i, sign in enumerate(signs):
                scaled = raw[i * rows : (i + 1) * rows] * (LOG2E * HEAD_DIM**-0.5)
                if hop < 2:
                    distance = jnp.abs(index + aheads[i])
                    score = scaled - slope * distance
                    if (hop + 1) * bins - 1 + SHIFT > RADIUS:
                        score = jnp.where(distance <= RADIUS, score, FAR)
                else:
                    signed = index * float(sign)
                    score = scaled - slope * signed
                    farthest = begin + CHUNK - 1 if sign > 0 else bins - 1 - begin
                    if hop * bins + farthest + SHIFT > RADIUS:
                        score = jnp.where(signed <= RADIUS - aheads[i], score, FAR)
                score_ref[buffer, i * rows : (i + 1) * rows, begin : begin + CHUNK] = score
                for lanes in range(0, CHUNK, LANES):
                    piece = score[:, lanes : lanes + LANES]
                    tops[i] = piece if tops[i] is None else jnp.maximum(tops[i], piece)
        peaks = [
            jnp.maximum(jnp.max(top, axis=1, keepdims=True), 0.1 * FAR) for top in tops
        ]
        totals = [None] * count
        gained = None
        for begin in range(0, bins, CHUNK):
            weights = []
            for i in range(count):
                exps = jnp.exp2(
                    score_ref[buffer, i * rows : (i + 1) * rows, begin : begin + CHUNK] - peaks[i]
                )
                for lanes in range(0, CHUNK, LANES):
                    piece = exps[:, lanes : lanes + LANES]
                    totals[i] = piece if totals[i] is None else totals[i] + piece
                weights.append(exps.astype(jnp.bfloat16))
            term = jnp.dot(
                jnp.concatenate(weights, axis=0) if count > 1 else weights[0],
                v_ref[begin : begin + CHUNK, start:stop],
                preferred_element_type=jnp.float32,
            )
            gained = term if gained is None else gained + term
        for i, slot in enumerate(slots):
            peak = peaks[i] - slope * aheads[i] if hop >= 2 else peaks[i]
            stat_ref[slot, head : head + 1, :] = as_row(peak)
            stat_ref[slot, groups + head : groups + head + 1, :] = as_row(
                jnp.sum(totals[i], axis=1, keepdims=True)
            )
            for tile in range(start, stop, LANES):
                parts[i].setdefault(tile, []).append(
                    (first, gained[i * rows : (i + 1) * rows, tile - start : tile - start + LANES])
                )
    for i, slot in enumerate(slots):
        for tile, pieces in parts[i].items():
            lane = lax.broadcasted_iota(jnp.int32, (rows, LANES), 1) + tile
            value = pieces[0][1]
            for first, piece in pieces[1:]:
                value = jnp.where(lane >= first, piece, value)
            out_ref[slot, :, tile : tile + LANES] = value.astype(jnp.bfloat16)


def attend_kernel(
    hops, seq_count, head_count,
    query_ref, type_ref, promoter_ref, offset_ref, embed_ref, k_hbm, v_hbm, w_hbm, slope_ref,
    result_ref,
    k_ref, v_ref, w_ref, pack_ref, out_ref, stat_ref, back_ref, back_stat_ref,
    score_ref, sum_ref, part_ref, head_ref,
    load_sem, q_send, q_recv, o_send, o_recv, s_send, s_recv, h_send, h_recv,
):
    position = lax.axis_index("seq")
    mine = lax.axis_index("head")
    rows, width = out_ref.shape[1:]
    groups = width // HEAD_DIM
    piece = result_ref.shape[1]
    loads = [
        pltpu.make_async_copy(src, dst, load_sem.at[i])
        for i, (src, dst) in enumerate(((k_hbm, k_ref), (v_hbm, v_ref), (w_hbm, w_ref)))
    ]
    for load in loads:
        load.start()

    def inside(index):
        return (index >= 0) & (index < seq_count)

    barrier = pltpu.get_barrier_semaphore()
    offsets = [sign * hop for hop in range(1, hops + 1) for sign in (1, -1)]
    for d in offsets:

        @pl.when(inside(position + d))
        def _(d=d):
            pl.semaphore_signal(
                barrier, inc=1, device_id=(position + d, mine), device_id_type=MESH
            )

    for r in range(1, head_count):
        pl.semaphore_signal(
            barrier, inc=1, device_id=(position, lax.rem(mine + r, head_count)), device_id_type=MESH
        )

    bins = k_ref.shape[0]
    chosen = (
        lax.broadcasted_iota(jnp.int32, (embed_ref.shape[0], rows), 0) == type_ref[...]
    ).astype(jnp.float32)
    embedded = jnp.dot(
        chosen.T.astype(jnp.bfloat16), embed_ref[...], preferred_element_type=jnp.float32
    )
    home = pack_ref.at[hops]
    home[:rows, :] = (query_ref[...].astype(jnp.float32) + embedded).astype(jnp.bfloat16)
    within = promoter_ref[...] + offset_ref[...] - position * bins
    high = lax.shift_right_arithmetic(within, 8)
    digit = lax.broadcasted_iota(jnp.int32, (EXTRA, rows), 0)
    corner = jnp.where(digit == 0, high, within - 256 * high).astype(jnp.float32)
    home[rows:, :] = jnp.zeros((EXTRA, width), jnp.bfloat16)
    home[rows:, :rows] = corner.astype(jnp.bfloat16)

    around = jnp.minimum(position, hops) + jnp.minimum(seq_count - 1 - position, hops)
    pl.semaphore_wait(barrier, around + head_count - 1)

    def query_copy(slot, target):
        return pltpu.make_async_remote_copy(
            src_ref=pack_ref.at[hops], dst_ref=pack_ref.at[slot], send_sem=q_send.at[slot],
            recv_sem=q_recv.at[slot], device_id=(target, mine), device_id_type=MESH,
        )

    def out_copy(slot, target):
        return pltpu.make_async_remote_copy(
            src_ref=out_ref.at[slot], dst_ref=back_ref.at[slot], send_sem=o_send.at[slot],
            recv_sem=o_recv.at[slot], device_id=(target, mine), device_id_type=MESH,
        )

    def stat_copy(slot, target):
        return pltpu.make_async_remote_copy(
            src_ref=stat_ref.at[slot], dst_ref=back_stat_ref.at[slot], send_sem=s_send.at[slot],
            recv_sem=s_recv.at[slot], device_id=(target, mine), device_id_type=MESH,
        )

    order = [1] + list(range(hops, 1, -1))
    for hop in order:
        for d in (hop, -hop):

            @pl.when(inside(position + d))
            def _(d=d):
                query_copy(d + hops, position + d).start()

    for d in offsets:

        @pl.when(jnp.logical_not(inside(position - d)))
        def _(d=d):
            pack_ref[d + hops] = jnp.zeros((rows + EXTRA, width), jnp.bfloat16)

    loads[0].wait()
    loads[1].wait()

    for hop in order:
        pair = (hop, -hop)
        for d in pair:

            @pl.when(inside(position - d))
            def _(d=d):
                query_copy(d + hops, position - d).wait_recv()

        @pl.when(inside(position - hop) | inside(position + hop))
        def _(hop=hop, pair=pair):
            attend(
                hop, (1, -1), [d + hops for d in pair], pack_ref, k_ref, v_ref, slope_ref,
                score_ref, out_ref, stat_ref,
            )

        for d in pair:

            @pl.when(inside(position - d))
            def _(d=d):
                stat_copy(d + hops, position - d).start()
                out_copy(d + hops, position - d).start()

    attend(
        0, (1,), [hops], pack_ref, k_ref, v_ref, slope_ref, score_ref, out_ref, stat_ref
    )

    back_stat_ref[hops] = stat_ref[hops]
    for d in offsets:
        slot = d + hops

        @pl.when(inside(position + d))
        def _(d=d, slot=slot):
            stat_copy(slot, position + d).wait_recv()

        @pl.when(jnp.logical_not(inside(position + d)))
        def _(slot=slot):
            back_stat_ref[slot, :groups, :] = jnp.full((groups, rows), FAR, jnp.float32)
            back_stat_ref[slot, groups:, :] = jnp.zeros((groups, rows), jnp.float32)

    slots = 2 * hops + 1
    peak = back_stat_ref[0, :groups, :]
    for slot in range(1, slots):
        peak = jnp.maximum(peak, back_stat_ref[slot, :groups, :])
    factors = [jnp.exp2(back_stat_ref[slot, :groups, :] - peak) for slot in range(slots)]
    total = factors[0] * back_stat_ref[0, groups:, :]
    for slot in range(1, slots):
        total = total + factors[slot] * back_stat_ref[slot, groups:, :]
    lane = lax.broadcasted_iota(jnp.int32, (rows, width), 1)

    def spread(factor):
        columns = factor.T
        wide = columns[:, 0:1]
        for head in range(1, groups):
            wide = jnp.where(lane >= head * HEAD_DIM, columns[:, head : head + 1], wide)
        return wide

    sum_ref[...] = out_ref[hops].astype(jnp.float32) * spread(factors[hops] / total)
    for d in offsets:
        slot = d + hops

        @pl.when(inside(position + d))
        def _(d=d, slot=slot):
            out_copy(slot, position + d).wait_recv()
            sum_ref[...] += back_ref[slot].astype(jnp.float32) * spread(factors[slot] / total)

    pooled = sum_ref[...].astype(jnp.bfloat16)
    loads[2].wait()

    def head_copy(r, target):
        return pltpu.make_async_remote_copy(
            src_ref=part_ref.at[r - 1], dst_ref=head_ref.at[r - 1], send_sem=h_send.at[r - 1],
            recv_sem=h_recv.at[r - 1], device_id=(position, target), device_id_type=MESH,
        )

    def share(target):
        columns = pl.ds(pl.multiple_of(target * piece, piece), piece)
        return jnp.dot(pooled, w_ref[:, columns], preferred_element_type=jnp.float32)

    for r in range(1, head_count):
        target = lax.rem(mine + r, head_count)
        part_ref[r - 1] = share(target).astype(jnp.bfloat16)
        head_copy(r, target).start()
    result = share(mine)
    for r in range(1, head_count):
        head_copy(r, lax.rem(mine + r, head_count)).wait_recv()
        result = result + head_ref[r - 1].astype(jnp.float32)
    result_ref[...] = result

    for r in range(1, head_count):
        head_copy(r, lax.rem(mine + r, head_count)).wait_send()
    for d in offsets:

        @pl.when(inside(position + d))
        def _(d=d):
            query_copy(d + hops, position + d).wait_send()

        @pl.when(inside(position - d))
        def _(d=d):
            stat_copy(d + hops, position - d).wait_send()
            out_copy(d + hops, position - d).wait_send()


def local(queries, cell_types, promoters, offsets, cell_embed, bin_keys, bin_values, slopes, w_out):
    seq_count = lax.axis_size("seq")
    bins = bin_keys.shape[0]
    rows, width = queries.shape
    groups = slopes.shape[0]
    hops = min(HOPS, seq_count - 1)
    head_count = lax.axis_size("head")
    slots = 2 * hops + 1
    piece = w_out.shape[1] // head_count
    vmem = pl.BlockSpec(memory_space=pltpu.VMEM)
    anywhere = pl.BlockSpec(memory_space=pl.ANY)
    result = pl.pallas_call(
        functools.partial(attend_kernel, hops, seq_count, head_count),
        out_shape=jax.ShapeDtypeStruct((rows, piece), jnp.float32),
        in_specs=[vmem] * 5 + [anywhere] * 3 + [pl.BlockSpec(memory_space=pltpu.SMEM)],
        out_specs=vmem,
        scratch_shapes=[
            pltpu.VMEM((bins, width), jnp.bfloat16),
            pltpu.VMEM((bins, width), jnp.bfloat16),
            pltpu.VMEM(w_out.shape, jnp.bfloat16),
            pltpu.VMEM((slots, rows + EXTRA, width), jnp.bfloat16),
            pltpu.VMEM((slots, rows, width), jnp.bfloat16),
            pltpu.VMEM((slots, 2 * groups, rows), jnp.float32),
            pltpu.VMEM((slots, rows, width), jnp.bfloat16),
            pltpu.VMEM((slots, 2 * groups, rows), jnp.float32),
            pltpu.VMEM((2, 2 * rows, bins), jnp.float32),
            pltpu.VMEM((rows, width), jnp.float32),
            pltpu.VMEM((head_count - 1, rows, piece), jnp.bfloat16),
            pltpu.VMEM((head_count - 1, rows, piece), jnp.bfloat16),
            pltpu.SemaphoreType.DMA((3,)),
        ]
        + [pltpu.SemaphoreType.DMA((slots,))] * 6
        + [pltpu.SemaphoreType.DMA((head_count - 1,))] * 2,
        compiler_params=pltpu.CompilerParams(collective_id=0, has_side_effects=True),
    )(
        queries,
        cell_types[None],
        promoters[None],
        offsets[None],
        cell_embed,
        bin_keys,
        bin_values,
        w_out,
        slopes,
    )
    return result.astype(jnp.bfloat16)


def solution(mesh):
    return jax.shard_map(
        local,
        mesh=mesh,
        in_specs=(
            P("seq", "head"),
            P("seq"),
            P("seq"),
            P("seq"),
            P(None, "head"),
            P("seq", "head"),
            P("seq", "head"),
            P("head"),
            P("head", None),
        ),
        out_specs=P("seq", "head"),
        check_vma=False,
    )
```

```python
import functools

import jax
import jax.numpy as jnp
from jax import lax
from jax.experimental import pallas as pl
from jax.experimental.pallas import tpu as pltpu
from jax.sharding import PartitionSpec as P

HEAD_DIM = 96
RADIUS = 7812
SHIFT = 64
HOPS = 4
LANES = 128
CHUNK = 256
EXTRA = 16
LOG2E = 1.4426950408889634
FAR = -1e30


MESH = pl.DeviceIdType.MESH


def identity_mask(size):
    return lax.broadcasted_iota(jnp.int32, (size, size), 0) == lax.broadcasted_iota(
        jnp.int32, (size, size), 1
    )


def as_column(row):
    size = row.shape[1]
    return jnp.sum(jnp.where(identity_mask(size), row, 0.0), axis=1, keepdims=True)


def as_row(column):
    size = column.shape[0]
    return jnp.sum(jnp.where(identity_mask(size), column, 0.0), axis=0, keepdims=True)


def tiles_of(head):
    first = head * HEAD_DIM
    start = first // LANES * LANES
    stop = -(-(first + HEAD_DIM) // LANES) * LANES
    return first, start, stop


def attend(hop, signs, slots, pack_ref, k_ref, v_ref, slope_ref, score_ref, out_ref, stat_ref):
    bins = k_ref.shape[0]
    rows = pack_ref.shape[1] - EXTRA
    width = k_ref.shape[1]
    groups = width // HEAD_DIM
    count = len(signs)
    aheads = []
    for sign, slot in zip(signs, slots):
        corner = pack_ref[slot, rows:, :rows].astype(jnp.float32)
        within = as_column(corner[0:1] * 256.0 + corner[1:2])
        aheads.append(hop * bins - sign * within if hop >= 2 else sign * hop * bins - within)
    parts = [{} for _ in signs]
    for head in range(groups):
        first, start, stop = tiles_of(head)
        slope = slope_ref[head] * LOG2E
        lane = lax.broadcasted_iota(jnp.int32, (count * rows, stop - start), 1) + start
        query = [pack_ref[slot, :rows, start:stop] for slot in slots]
        query = jnp.concatenate(query, axis=0) if count > 1 else query[0]
        query = jnp.where((lane >= first) & (lane < first + HEAD_DIM), query, jnp.zeros_like(query))
        buffer = head % 2
        tops = [None] * count
        for begin in range(0, bins, CHUNK):
            raw = lax.dot_general(
                query,
                k_ref[begin : begin + CHUNK, start:stop],
                (((1,), (1,)), ((), ())),
                preferred_element_type=jnp.float32,
            )
            index = (lax.broadcasted_iota(jnp.int32, (1, CHUNK), 1) + begin).astype(jnp.float32)
            for i, sign in enumerate(signs):
                scaled = raw[i * rows : (i + 1) * rows] * (LOG2E * HEAD_DIM**-0.5)
                if hop < 2:
                    distance = jnp.abs(index + aheads[i])
                    score = scaled - slope * distance
                    if (hop + 1) * bins - 1 + SHIFT > RADIUS:
                        score = jnp.where(distance <= RADIUS, score, FAR)
                else:
                    signed = index * float(sign)
                    score = scaled - slope * signed
                    farthest = begin + CHUNK - 1 if sign > 0 else bins - 1 - begin
                    if hop * bins + farthest + SHIFT > RADIUS:
                        score = jnp.where(signed <= RADIUS - aheads[i], score, FAR)
                score_ref[buffer, i * rows : (i + 1) * rows, begin : begin + CHUNK] = score
                for lanes in range(0, CHUNK, LANES):
                    piece = score[:, lanes : lanes + LANES]
                    tops[i] = piece if tops[i] is None else jnp.maximum(tops[i], piece)
        peaks = [
            jnp.maximum(jnp.max(top, axis=1, keepdims=True), 0.1 * FAR) for top in tops
        ]
        totals = [None] * count
        gained = None
        for begin in range(0, bins, CHUNK):
            weights = []
            for i in range(count):
                exps = jnp.exp2(
                    score_ref[buffer, i * rows : (i + 1) * rows, begin : begin + CHUNK] - peaks[i]
                )
                for lanes in range(0, CHUNK, LANES):
                    piece = exps[:, lanes : lanes + LANES]
                    totals[i] = piece if totals[i] is None else totals[i] + piece
                weights.append(exps.astype(jnp.bfloat16))
            term = jnp.dot(
                jnp.concatenate(weights, axis=0) if count > 1 else weights[0],
                v_ref[begin : begin + CHUNK, start:stop],
                preferred_element_type=jnp.float32,
            )
            gained = term if gained is None else gained + term
        for i, slot in enumerate(slots):
            peak = peaks[i] - slope * aheads[i] if hop >= 2 else peaks[i]
            stat_ref[slot, head : head + 1, :] = as_row(peak)
            stat_ref[slot, groups + head : groups + head + 1, :] = as_row(
                jnp.sum(totals[i], axis=1, keepdims=True)
            )
            for tile in range(start, stop, LANES):
                parts[i].setdefault(tile, []).append(
                    (first, gained[i * rows : (i + 1) * rows, tile - start : tile - start + LANES])
                )
    for i, slot in enumerate(slots):
        for tile, pieces in parts[i].items():
            lane = lax.broadcasted_iota(jnp.int32, (rows, LANES), 1) + tile
            value = pieces[0][1]
            for first, piece in pieces[1:]:
                value = jnp.where(lane >= first, piece, value)
            out_ref[slot, :, tile : tile + LANES] = value.astype(jnp.bfloat16)


def attend_kernel(
    hops, seq_count, head_count,
    query_ref, type_ref, promoter_ref, offset_ref, embed_ref, k_hbm, v_hbm, w_hbm, slope_ref,
    result_ref,
    k_ref, v_ref, w_ref, pack_ref, out_ref, stat_ref, back_ref, back_stat_ref,
    score_ref, sum_ref, part_ref, head_ref,
    load_sem, q_send, q_recv, o_send, o_recv, s_send, s_recv, h_send, h_recv,
):
    position = lax.axis_index("seq")
    mine = lax.axis_index("head")
    rows, width = out_ref.shape[1:]
    groups = width // HEAD_DIM
    piece = result_ref.shape[1]
    loads = [
        pltpu.make_async_copy(src, dst, load_sem.at[i])
        for i, (src, dst) in enumerate(((k_hbm, k_ref), (v_hbm, v_ref), (w_hbm, w_ref)))
    ]
    for load in loads:
        load.start()

    def inside(index):
        return (index >= 0) & (index < seq_count)

    barrier = pltpu.get_barrier_semaphore()
    offsets = [sign * hop for hop in range(1, hops + 1) for sign in (1, -1)]
    for d in offsets:

        @pl.when(inside(position + d))
        def _(d=d):
            pl.semaphore_signal(
                barrier, inc=1, device_id=(position + d, mine), device_id_type=MESH
            )

    for r in range(1, head_count):
        pl.semaphore_signal(
            barrier, inc=1, device_id=(position, lax.rem(mine + r, head_count)), device_id_type=MESH
        )

    bins = k_ref.shape[0]
    chosen = (
        lax.broadcasted_iota(jnp.int32, (embed_ref.shape[0], rows), 0) == type_ref[...]
    ).astype(jnp.float32)
    embedded = jnp.dot(
        chosen.T.astype(jnp.bfloat16), embed_ref[...], preferred_element_type=jnp.float32
    )
    home = pack_ref.at[hops]
    home[:rows, :] = (query_ref[...].astype(jnp.float32) + embedded).astype(jnp.bfloat16)
    within = promoter_ref[...] + offset_ref[...] - position * bins
    high = lax.shift_right_arithmetic(within, 8)
    digit = lax.broadcasted_iota(jnp.int32, (EXTRA, rows), 0)
    corner = jnp.where(digit == 0, high, within - 256 * high).astype(jnp.float32)
    home[rows:, :] = jnp.zeros((EXTRA, width), jnp.bfloat16)
    home[rows:, :rows] = corner.astype(jnp.bfloat16)

    around = jnp.minimum(position, hops) + jnp.minimum(seq_count - 1 - position, hops)
    pl.semaphore_wait(barrier, around + head_count - 1)

    side = 1 - 2 * lax.rem(position, 2)
    partner = position + side

    def query_copy(source, slot, target, send):
        return pltpu.make_async_remote_copy(
            src_ref=pack_ref.at[source], dst_ref=pack_ref.at[slot], send_sem=q_send.at[send],
            recv_sem=q_recv.at[slot], device_id=(target, mine), device_id_type=MESH,
        )

    sends = [
        (True, lambda: query_copy(hops, hops + side, partner, 0)),
        (inside(position + 2), lambda: query_copy(hops, hops + 2, position + 2, 1)),
        (inside(position - 2), lambda: query_copy(hops, hops - 2, position - 2, 2)),
    ]
    onward, final = [], []
    for s, send in ((1, 3), (-1, 5)):
        onward += [
            (
                inside(position - 2 * s) & inside(position + 2 * s),
                lambda s=s, send=send: query_copy(
                    hops + 2 * s, hops + 4 * s, position + 2 * s, send
                ),
            ),
            (
                inside(position - 2 * s),
                lambda s=s, send=send: query_copy(
                    hops + 2 * s, hops + 2 * s + side, partner, send + 1
                ),
            ),
        ]
        final.append(
            (
                inside(position - 4 * s) & (side == -s),
                lambda s=s: query_copy(hops + 4 * s, hops + 3 * s, partner, 7),
            )
        )

    def each(entries, act):
        for condition, make in entries:
            if condition is True:
                act(make())
            else:

                @pl.when(condition)
                def _(make=make):
                    act(make())

    def arrived(d):
        @pl.when(inside(position - d))
        def _():
            query_copy(hops, d + hops, partner, 0).wait_recv()

    def out_copy(slot, target):
        return pltpu.make_async_remote_copy(
            src_ref=out_ref.at[slot], dst_ref=back_ref.at[slot], send_sem=o_send.at[slot],
            recv_sem=o_recv.at[slot], device_id=(target, mine), device_id_type=MESH,
        )

    def stat_copy(slot, target):
        return pltpu.make_async_remote_copy(
            src_ref=stat_ref.at[slot], dst_ref=back_stat_ref.at[slot], send_sem=s_send.at[slot],
            recv_sem=s_recv.at[slot], device_id=(target, mine), device_id_type=MESH,
        )

    each(sends, lambda copy: copy.start())

    for d in offsets:

        @pl.when(jnp.logical_not(inside(position - d)))
        def _(d=d):
            pack_ref[d + hops] = jnp.zeros((rows + EXTRA, width), jnp.bfloat16)

    loads[0].wait()
    loads[1].wait()

    arrived(2)
    arrived(-2)
    each(onward, lambda copy: copy.start())
    for hop in (2, 1, 4, 3):
        pair = (hop, -hop)
        if hop == 1:
            arrived(4)
            arrived(-4)
            each(final, lambda copy: copy.start())
        if hop in (1, 3):
            for d in pair:
                arrived(d)

        @pl.when(inside(position - hop) | inside(position + hop))
        def _(hop=hop, pair=pair):
            attend(
                hop, (1, -1), [d + hops for d in pair], pack_ref, k_ref, v_ref, slope_ref,
                score_ref, out_ref, stat_ref,
            )

        for d in pair:

            @pl.when(inside(position - d))
            def _(d=d):
                stat_copy(d + hops, position - d).start()
                out_copy(d + hops, position - d).start()

    attend(
        0, (1,), [hops], pack_ref, k_ref, v_ref, slope_ref, score_ref, out_ref, stat_ref
    )

    back_stat_ref[hops] = stat_ref[hops]
    for d in offsets:
        slot = d + hops

        @pl.when(inside(position + d))
        def _(d=d, slot=slot):
            stat_copy(slot, position + d).wait_recv()

        @pl.when(jnp.logical_not(inside(position + d)))
        def _(slot=slot):
            back_stat_ref[slot, :groups, :] = jnp.full((groups, rows), FAR, jnp.float32)
            back_stat_ref[slot, groups:, :] = jnp.zeros((groups, rows), jnp.float32)

    slots = 2 * hops + 1
    peak = back_stat_ref[0, :groups, :]
    for slot in range(1, slots):
        peak = jnp.maximum(peak, back_stat_ref[slot, :groups, :])
    factors = [jnp.exp2(back_stat_ref[slot, :groups, :] - peak) for slot in range(slots)]
    total = factors[0] * back_stat_ref[0, groups:, :]
    for slot in range(1, slots):
        total = total + factors[slot] * back_stat_ref[slot, groups:, :]
    lane = lax.broadcasted_iota(jnp.int32, (rows, width), 1)

    def spread(factor):
        columns = factor.T
        wide = columns[:, 0:1]
        for head in range(1, groups):
            wide = jnp.where(lane >= head * HEAD_DIM, columns[:, head : head + 1], wide)
        return wide

    sum_ref[...] = out_ref[hops].astype(jnp.float32) * spread(factors[hops] / total)
    for d in offsets:
        slot = d + hops

        @pl.when(inside(position + d))
        def _(d=d, slot=slot):
            out_copy(slot, position + d).wait_recv()
            sum_ref[...] += back_ref[slot].astype(jnp.float32) * spread(factors[slot] / total)

    pooled = sum_ref[...].astype(jnp.bfloat16)
    loads[2].wait()

    def head_copy(r, target):
        return pltpu.make_async_remote_copy(
            src_ref=part_ref.at[r - 1], dst_ref=head_ref.at[r - 1], send_sem=h_send.at[r - 1],
            recv_sem=h_recv.at[r - 1], device_id=(position, target), device_id_type=MESH,
        )

    def share(target):
        columns = pl.ds(pl.multiple_of(target * piece, piece), piece)
        return jnp.dot(pooled, w_ref[:, columns], preferred_element_type=jnp.float32)

    for r in range(1, head_count):
        target = lax.rem(mine + r, head_count)
        part_ref[r - 1] = share(target).astype(jnp.bfloat16)
        head_copy(r, target).start()
    result = share(mine)
    for r in range(1, head_count):
        head_copy(r, lax.rem(mine + r, head_count)).wait_recv()
        result = result + head_ref[r - 1].astype(jnp.float32)
    result_ref[...] = result

    each(sends + onward + final, lambda copy: copy.wait_send())
    for r in range(1, head_count):
        head_copy(r, lax.rem(mine + r, head_count)).wait_send()
    for d in offsets:

        @pl.when(inside(position - d))
        def _(d=d):
            stat_copy(d + hops, position - d).wait_send()
            out_copy(d + hops, position - d).wait_send()


def local(queries, cell_types, promoters, offsets, cell_embed, bin_keys, bin_values, slopes, w_out):
    seq_count = lax.axis_size("seq")
    bins = bin_keys.shape[0]
    rows, width = queries.shape
    groups = slopes.shape[0]
    hops = min(HOPS, seq_count - 1)
    head_count = lax.axis_size("head")
    slots = 2 * hops + 1
    piece = w_out.shape[1] // head_count
    vmem = pl.BlockSpec(memory_space=pltpu.VMEM)
    anywhere = pl.BlockSpec(memory_space=pl.ANY)
    result = pl.pallas_call(
        functools.partial(attend_kernel, hops, seq_count, head_count),
        out_shape=jax.ShapeDtypeStruct((rows, piece), jnp.float32),
        in_specs=[vmem] * 5 + [anywhere] * 3 + [pl.BlockSpec(memory_space=pltpu.SMEM)],
        out_specs=vmem,
        scratch_shapes=[
            pltpu.VMEM((bins, width), jnp.bfloat16),
            pltpu.VMEM((bins, width), jnp.bfloat16),
            pltpu.VMEM(w_out.shape, jnp.bfloat16),
            pltpu.VMEM((slots, rows + EXTRA, width), jnp.bfloat16),
            pltpu.VMEM((slots, rows, width), jnp.bfloat16),
            pltpu.VMEM((slots, 2 * groups, rows), jnp.float32),
            pltpu.VMEM((slots, rows, width), jnp.bfloat16),
            pltpu.VMEM((slots, 2 * groups, rows), jnp.float32),
            pltpu.VMEM((2, 2 * rows, bins), jnp.float32),
            pltpu.VMEM((rows, width), jnp.float32),
            pltpu.VMEM((head_count - 1, rows, piece), jnp.bfloat16),
            pltpu.VMEM((head_count - 1, rows, piece), jnp.bfloat16),
            pltpu.SemaphoreType.DMA((3,)),
        ]
        + [pltpu.SemaphoreType.DMA((slots,))] * 6
        + [pltpu.SemaphoreType.DMA((head_count - 1,))] * 2,
        compiler_params=pltpu.CompilerParams(collective_id=0, has_side_effects=True),
    )(
        queries,
        cell_types[None],
        promoters[None],
        offsets[None],
        cell_embed,
        bin_keys,
        bin_values,
        w_out,
        slopes,
    )
    return result.astype(jnp.bfloat16)


def solution(mesh):
    return jax.shard_map(
        local,
        mesh=mesh,
        in_specs=(
            P("seq", "head"),
            P("seq"),
            P("seq"),
            P("seq"),
            P(None, "head"),
            P("seq", "head"),
            P("seq", "head"),
            P("head"),
            P("head", None),
        ),
        out_specs=P("seq", "head"),
        check_vma=False,
    )
```
